32 devices in a mesh: dom: 16 (over z, y, x), row: 2 (over core).
Axes of the slice: x: 2, y: 2, z: 4, core: 2. Of those that a mesh axis runs over, the one named last changes fastest.
Arguments:
- scatter: bfloat16 [16, 2, 3, 4, 256, 1024], P('dom', None, None, 'row'), may hold values from -0.125 to 0.125
- pattern: int32 [16, 3, 4, 4], P('dom', None, 'row'), may hold values 0 or 1
- source: bfloat16 [16, 2, 3, 16, 4, 256], P('dom', None, None, None, 'row'), may hold values from -6 to 6
Outputs:
- outgoing_traces: bfloat16 [16, 2, 3, 16, 4, 256], P('dom', None, None, None, 'row')
The draws below stay inside these ranges and needn't reach their ends.
All inputs are finite; a program needn't handle non-finite values. No bound on the sum of `pattern` on one device may be relied on, other than what follows from the above.
Results may differ from the reference program's by a relative error of at most 0.0095.
Values may be sent and summed in bfloat16 or wider, within the bound.
No kernel may reach another device: no remote copies, remote signals or barrier semaphores. Data moves between devices by JAX's collectives and lax.ppermute only.
A program may use at most 64 MiB of HBM per device.

```python
import jax
import jax.numpy as jnp
from jax import lax

NT = 3
FACE = 256
FACES = 4
ILLUM = 16
ITERS = 8
NL = 16


def touch_ends(values, own_key, smallest, high):
    index_at = [jax.random.randint(jax.random.fold_in(own_key, axis), (), 0, length) for axis, length in enumerate(values.shape)]
    widest = values.shape.index(max(values.shape))
    next_to = index_at[:widest] + [(index_at[widest] + 1) % values.shape[widest]] + index_at[widest + 1:]
    return values.at[tuple(index_at)].set(smallest).at[tuple(next_to)].set(high)


def levels(stream_key, shape, cuts, low, top_value):
    factor_of = 1.0
    for axis_at, parts in cuts:
        steps = jax.random.uniform(jax.random.fold_in(jax.random.fold_in(stream_key, 6), axis_at), (parts,), jnp.float32, low / len(cuts), top_value / len(cuts))
        factor_of = factor_of * jnp.repeat(jnp.exp(steps), shape[axis_at] // parts).reshape((-1,) + (1,) * (len(shape) - 1 - axis_at))
    return factor_of


def gaussian(stream_key, shape, spread, limit, pieces=(), held_as=jnp.bfloat16):
    factor_of = levels(stream_key, shape, pieces, -0.22, 0.18) if pieces else 1.0
    array = jax.random.normal(stream_key, shape, jnp.float32) * spread * factor_of
    return jnp.minimum(jnp.maximum(array, -limit), limit).astype(held_as)


def setup_inputs(seed: int = 0) -> dict:
    splits = jax.random.split(jax.random.key(seed), 4)
    scatter = gaussian(splits[0], (NL, 2, NT, FACES, FACE, FACES * FACE), (8 * FACE) ** -0.5, 0.125, ((0, 16), (3, 2)))
    pattern = touch_ends((jax.random.randint(splits[1], (NL, NT, FACES, FACES), 0, 4) < 3).astype(jnp.int32), jax.random.fold_in(splits[1], 1), 0, 1)
    source = gaussian(splits[2], (NL, 2, NT, ILLUM, FACES, FACE), 1.0, 6.0, ((0, 16), (4, 2)))
    return {"scatter": scatter, "pattern": pattern, "source": source}


def incoming_of(outgoing):
    zero_column = jnp.zeros_like(outgoing[:1, :, :, :, 0])
    from_west = jnp.concatenate([zero_column, outgoing[:-1, :, :, :, 1]], axis=0)
    from_east = jnp.concatenate([outgoing[1:, :, :, :, 0], zero_column], axis=0)
    zero_layer = jnp.zeros_like(outgoing[:, :, :1, :, 0])
    from_south = jnp.concatenate([zero_layer, outgoing[:, :, :-1, :, 3]], axis=2)
    from_north = jnp.concatenate([outgoing[:, :, 1:, :, 2], zero_layer], axis=2)
    return jnp.stack([from_west, from_east, from_south, from_north], axis=4)


def contract(operators, vectors):
    return jnp.einsum("tfqk,tfjk->tjfq", operators, vectors)


def apply_column(packed):
    operator, pattern, incoming, source = packed
    weights = pattern.astype(jnp.bfloat16)[None, :, :, None, :, None]
    masked = (weights * incoming[:, :, None, :, :, :]).astype(jnp.bfloat16)
    masked = masked.astype(jnp.float32).reshape(2, NT, FACES, ILLUM, FACES * FACE)
    op_real = operator[0].astype(jnp.float32)
    op_imag = operator[1].astype(jnp.float32)
    real_part = contract(op_real, masked[0]) - contract(op_imag, masked[1]) + source[0].astype(jnp.float32)
    imag_part = contract(op_real, masked[1]) + contract(op_imag, masked[0]) + source[1].astype(jnp.float32)
    return jnp.stack([real_part, imag_part], axis=0).astype(jnp.bfloat16)


def reference(scatter, pattern, source):
    outgoing = source
    for sweep_index in range(ITERS):
        incoming = incoming_of(outgoing)
        outgoing = lax.map(apply_column, (scatter, pattern, incoming, source))
    return outgoing
```

```python
import functools

import jax
import jax.numpy as jnp
from jax import lax
from jax.experimental import pallas as pl
from jax.experimental.pallas import tpu as pltpu
from jax.sharding import PartitionSpec as P

ITERS = 8
F32 = jnp.float32
BF16 = jnp.bfloat16


def from_behind(value, axis, by):
    peers = lax.axis_size(axis)
    pairs = [(i, i + by) for i in range(peers) if 0 <= i + by < peers]
    return lax.ppermute(value, axis, pairs)


def horizontal(gathered, west_edge, east_edge):
    from_west = jnp.concatenate([west_edge[None], gathered[:-1, :, :, :, 1]], axis=0)
    from_east = jnp.concatenate([gathered[1:, :, :, :, 0], east_edge[None]], axis=0)
    return jnp.stack([from_west, from_east], axis=4)


def vertical(gathered):
    zero_layer = jnp.zeros_like(gathered[:, :, :1, :, 0])
    from_south = jnp.concatenate([zero_layer, gathered[:, :, :-1, :, 3]], axis=2)
    from_north = jnp.concatenate([gathered[:, :, 1:, :, 2], zero_layer], axis=2)
    return jnp.stack([from_south, from_north], axis=4)


def contract(operators, vectors):
    return jnp.einsum("ctfqk,ctfjk->ctjfq", operators, vectors, preferred_element_type=F32)


def apply_range(scatter, pattern, incoming):
    columns, layers, held, _ = pattern.shape
    count = incoming.shape[4]
    width = incoming.shape[5]
    weights = pattern.astype(BF16)[:, None, :, :, None, :, None]
    masked = weights * incoming[:, :, :, None, :, :, :]
    masked = masked.reshape(columns, 2, layers, held, incoming.shape[3], count * width)
    real_part = contract(scatter[:, 0], masked[:, 0]) - contract(scatter[:, 1], masked[:, 1])
    imag_part = contract(scatter[:, 0], masked[:, 1]) + contract(scatter[:, 1], masked[:, 0])
    return jnp.stack([real_part, imag_part], axis=1)


def edge_traces(gathered):
    columns = gathered.shape[0]
    west_edge = from_behind(gathered[columns - 1, :, :, :, 1], "dom", 1)
    east_edge = from_behind(gathered[0, :, :, :, 0], "dom", -1)
    return (west_edge, east_edge)


def general(scatter, pattern, source):
    outgoing = source
    for _ in range(ITERS):
        gathered = lax.all_gather(outgoing, "row", axis=4, tiled=True)
        west_edge, east_edge = edge_traces(gathered)
        incoming = jnp.concatenate(
            [horizontal(gathered, west_edge, east_edge), vertical(gathered)], axis=4
        )
        result = apply_range(scatter, pattern, incoming)
        outgoing = (result + source.astype(F32)).astype(BF16)
    return outgoing


def near(c, columns):
    return c ^ 1


def far(c, columns):
    other = c + 1 if c % 2 else c - 1
    return other if 0 <= other < columns else c


def to_same(partner, columns):
    def target(c, r):
        other = partner(c, columns)
        return (other, r) if other != c else (c, 1 - r)

    return pairs_of(target, columns)


def to_other(partner, columns):
    def target(c, r):
        return (partner(c, columns), 1) if r == 0 else (c, 0)

    return pairs_of(target, columns)


def pairs_of(target, columns):
    pairs = []
    for c in range(columns):
        for r in range(2):
            to_c, to_r = target(c, r)
            pairs.append((2 * c + r, 2 * to_c + to_r))
    return pairs


def swapped():
    return (lax.axis_index("row") == 0) & (lax.axis_index("dom") % 2 == 0)


def load_kernel(scatter_ref, pattern_ref, out_ref, raw_ref, sems):
    parts, layers, held, width, _ = raw_ref.shape
    columns = lax.axis_size("dom")
    column = lax.axis_index("dom")
    even = column % 2 == 0
    swap = swapped()

    def copy(t, f, p):
        return pltpu.make_async_copy(scatter_ref.at[p, t, f], raw_ref.at[p, t, f], sems.at[p, t, f])

    steps = [(t, f, p) for t in range(layers) for f in range(held) for p in range(parts)]
    for step in steps:
        copy(*step).start()
    for t, f, p in steps:
        copy(t, f, p).wait()
        slot = jnp.where(swap, 1 - f, f)
        for g in range(4):
            if (g == 2 and t == 0) or (g == 3 and t == layers - 1):
                continue
            tile = raw_ref[p, t, f, :, g * width : (g + 1) * width].T
            keep = pattern_ref[(t * held + f) * 4 + g] != 0
            if g == 0:
                keep = keep & (column > 0)
                block = jnp.where(even, 2, 1)
            elif g == 1:
                keep = keep & (column < columns - 1)
                block = jnp.where(even, 1, 2)
            else:
                block = 0 if g == 2 else 3
            out_ref[p, t, slot, block] = jnp.where(keep, tile, jnp.zeros_like(tile))


def step_kernel(op_ref, src_a, src_b, own_a, own_b, near0, near1, far0, far1, out_a, out_b, *, last):
    _, layers, held, _, width, _ = op_ref.shape
    row0 = lax.axis_index("row") == 0
    pick = lambda a, b: jnp.where(row0, a, b)
    for t in range(layers):
        blocks = []
        if t > 0:
            blocks.append([pick(far1[p, t - 1], own_b[p, t - 1]) for p in range(2)])
        blocks.append([pick(near0[p, t], near1[p, t]) for p in range(2)])
        blocks.append([pick(far0[p, t], far1[p, t]) for p in range(2)])
        if t < layers - 1:
            blocks.append([pick(near1[p, t + 1], own_a[p, t + 1]) for p in range(2)])
        lo = 0 if t > 0 else 1
        hi = lo + len(blocks)
        x_real = jnp.concatenate([jnp.concatenate([re, im], axis=0) for re, im in blocks], axis=1)
        x_imag = jnp.concatenate([jnp.concatenate([-im, re], axis=0) for re, im in blocks], axis=1)
        sums = []
        for slot in range(held):
            acc = jnp.dot(x_real, op_ref[0, t, slot, lo:hi].reshape(-1, width), preferred_element_type=F32)
            acc += jnp.dot(x_imag, op_ref[1, t, slot, lo:hi].reshape(-1, width), preferred_element_type=F32)
            src = (src_a, src_b)[slot]
            acc += jnp.concatenate([src[0, t], src[1, t]], axis=0).astype(F32)
            sums.append(acc.astype(BF16))
        lit = sums[0].shape[0] // 2
        if last:
            swap = swapped()
            sums = [jnp.where(swap, sums[1], sums[0]), jnp.where(swap, sums[0], sums[1])]
        for out, value in zip((out_a, out_b), sums):
            out[0, t] = value[:lit]
            out[1, t] = value[lit:]


VMEM = pl.BlockSpec(memory_space=pltpu.VMEM)


def load(scatter, pattern):
    parts, layers, held, width, _ = scatter.shape
    return pl.pallas_call(
        load_kernel,
        out_shape=pltpu.VMEM((parts, layers, held, 4, width, width), BF16),
        in_specs=[pl.BlockSpec(memory_space=pl.ANY), pl.BlockSpec(memory_space=pltpu.SMEM)],
        out_specs=VMEM,
        scratch_shapes=[pltpu.VMEM(scatter.shape, BF16), pltpu.SemaphoreType.DMA((parts, layers, held))],
        compiler_params=pltpu.CompilerParams(vmem_limit_bytes=24 << 20),
        name="load",
    )(scatter, pattern)


def step(operator, src, own, received, last):
    shape = jax.ShapeDtypeStruct(own[0].shape, BF16)
    return pl.pallas_call(
        functools.partial(step_kernel, last=last),
        out_shape=(shape, shape),
        in_specs=[VMEM] * 9,
        out_specs=(VMEM, VMEM),
        compiler_params=pltpu.CompilerParams(vmem_limit_bytes=16 << 20),
        name="last_step" if last else "step",
    )(operator, *src, *own, *received)


def paired(scatter, pattern, source):
    columns = lax.axis_size("dom")
    axes = ("dom", "row")
    perms = [to_same(near, columns), to_other(near, columns), to_same(far, columns), to_other(far, columns)]
    faces = jnp.transpose(source[0], (3, 0, 1, 2, 4))
    swap = swapped()
    src = (jnp.where(swap, faces[1], faces[0]), jnp.where(swap, faces[0], faces[1]))
    operator = load(scatter[0], pattern.reshape(-1))
    own = src
    for n in range(ITERS):
        sent = (own[0], own[0], own[1], own[1])
        received = []
        for value, perm in zip(sent, perms):
            received.append(lax.ppermute(value, axes, perm))
        own = step(operator, src, own, received, n == ITERS - 1)
    return jnp.transpose(jnp.stack(own), (1, 2, 3, 0, 4))[None]


def local(scatter, pattern, source):
    if lax.axis_size("row") == 2 and lax.axis_size("dom") % 2 == 0 and scatter.shape[0] == 1:
        return paired(scatter, pattern, source)
    return general(scatter, pattern, source)


def solution(mesh):
    return jax.shard_map(
        local,
        mesh=mesh,
        in_specs=(
            P("dom", None, None, "row", None, None),
            P("dom", None, "row", None),
            P("dom", None, None, None, "row", None),
        ),
        out_specs=P("dom", None, None, None, "row", None),
        check_vma=False,
    )
```

```python
import functools

import jax
import jax.numpy as jnp
from jax import lax
from jax.experimental import pallas as pl
from jax.experimental.pallas import tpu as pltpu
from jax.sharding import PartitionSpec as P


ITERS = 8
F32 = jnp.float32
BF16 = jnp.bfloat16


def from_behind(value, axis, by):
    peers = lax.axis_size(axis)
    pairs = [(i, i + by) for i in range(peers) if 0 <= i + by < peers]
    return lax.ppermute(value, axis, pairs)


def horizontal(gathered, west_edge, east_edge):
    from_west = jnp.concatenate([west_edge[None], gathered[:-1, :, :, :, 1]], axis=0)
    from_east = jnp.concatenate([gathered[1:, :, :, :, 0], east_edge[None]], axis=0)
    return jnp.stack([from_west, from_east], axis=4)


def vertical(gathered):
    zero_layer = jnp.zeros_like(gathered[:, :, :1, :, 0])
    from_south = jnp.concatenate([zero_layer, gathered[:, :, :-1, :, 3]], axis=2)
    from_north = jnp.concatenate([gathered[:, :, 1:, :, 2], zero_layer], axis=2)
    return jnp.stack([from_south, from_north], axis=4)


def contract(operators, vectors):
    return jnp.einsum("ctfqk,ctfjk->ctjfq", operators, vectors, preferred_element_type=F32)


def apply_range(scatter, pattern, incoming):
    columns, layers, held, _ = pattern.shape
    count = incoming.shape[4]
    width = incoming.shape[5]
    weights = pattern.astype(BF16)[:, None, :, :, None, :, None]
    masked = weights * incoming[:, :, :, None, :, :, :]
    masked = masked.reshape(columns, 2, layers, held, incoming.shape[3], count * width)
    real_part = contract(scatter[:, 0], masked[:, 0]) - contract(scatter[:, 1], masked[:, 1])
    imag_part = contract(scatter[:, 0], masked[:, 1]) + contract(scatter[:, 1], masked[:, 0])
    return jnp.stack([real_part, imag_part], axis=1)


def edge_traces(gathered):
    columns = gathered.shape[0]
    west_edge = from_behind(gathered[columns - 1, :, :, :, 1], "dom", 1)
    east_edge = from_behind(gathered[0, :, :, :, 0], "dom", -1)
    return (west_edge, east_edge)


def general(scatter, pattern, source):
    outgoing = source
    for _ in range(ITERS):
        gathered = lax.all_gather(outgoing, "row", axis=4, tiled=True)
        west_edge, east_edge = edge_traces(gathered)
        incoming = jnp.concatenate(
            [horizontal(gathered, west_edge, east_edge), vertical(gathered)], axis=4
        )
        result = apply_range(scatter, pattern, incoming)
        outgoing = (result + source.astype(F32)).astype(BF16)
    return outgoing


def near(c, columns):
    return c ^ 1


def far(c, columns):
    other = c + 1 if c % 2 else c - 1
    return other if 0 <= other < columns else c


def to_same(partner, columns, stride):
    def target(c, r):
        other = partner(c, columns)
        if r == 0:
            return (other, 0) if other != c else (c, 1)
        beside = c ^ stride
        return (beside, 1) if partner(beside, columns) != beside else (beside, 0)

    return pairs_of(target, columns)


def to_other(partner, columns):
    def target(c, r):
        return (partner(c, columns), 1) if r == 0 else (c, 0)

    return pairs_of(target, columns)


def pairs_of(target, columns):
    pairs = []
    for c in range(columns):
        for r in range(2):
            to_c, to_r = target(c, r)
            pairs.append((2 * c + r, 2 * to_c + to_r))
    return pairs


def swapped():
    return (lax.axis_index("row") == 0) & (lax.axis_index("dom") % 2 == 0)


def load_kernel(scatter_ref, pattern_ref, early_ref, late_ref, raw_ref, sems):
    parts, layers, held, width, _ = raw_ref.shape
    columns = lax.axis_size("dom")
    column = lax.axis_index("dom")
    even = column % 2 == 0
    swap = swapped()

    def copy(t, f, p):
        return pltpu.make_async_copy(scatter_ref.at[p, t, f], raw_ref.at[p, t, f], sems.at[p, t, f])

    steps = [(t, f, p) for t in range(layers) for f in range(held) for p in range(parts)]
    for step in steps:
        copy(*step).start()
    for t, f, p in steps:
        copy(t, f, p).wait()
        slot = jnp.where(swap, 1 - f, f)

        def put(ref, block, g, keep):
            tile = raw_ref[p, t, f, :, pl.ds(pl.multiple_of(g * width, width), width)].T
            keep = keep & (pattern_ref[t, f, g] != 0)
            ref[p, t, slot, block] = jnp.where(keep, tile, jnp.zeros_like(tile))

        west = jnp.int32(0)
        near_face = jnp.where(even, west + 1, west)
        inside = jnp.where(even, column > 0, column < columns - 1)
        if t < layers - 1:
            put(early_ref, 0, 3, True)
        if t > 0:
            put(early_ref, 1, 2, True)
        put(late_ref, 0, near_face, True)
        put(late_ref, 1, 1 - near_face, inside)


def complex_dot(op_ref, t, slot, lo, hi, x_real, x_imag):
    width = op_ref.shape[-1]
    acc = jnp.dot(x_real, op_ref[0, t, slot, lo:hi].reshape(-1, width), preferred_element_type=F32)
    return acc + jnp.dot(x_imag, op_ref[1, t, slot, lo:hi].reshape(-1, width), preferred_element_type=F32)


def stacked(blocks):
    x_real = jnp.concatenate([jnp.concatenate([re, im], axis=0) for re, im in blocks], axis=1)
    x_imag = jnp.concatenate([jnp.concatenate([-im, re], axis=0) for re, im in blocks], axis=1)
    return x_real, x_imag


def early_kernel(op_ref, src_a, src_b, own, other, sum_ref):
    _, layers, held, _, _, _ = op_ref.shape
    row0 = lax.axis_index("row") == 0
    for t in range(layers):
        blocks = []
        if t < layers - 1:
            blocks.append([jnp.where(row0, other[0, p, t + 1], own[0, p, t + 1]) for p in range(2)])
        if t > 0:
            blocks.append([jnp.where(row0, other[1, p, t - 1], own[1, p, t - 1]) for p in range(2)])
        x_real, x_imag = stacked(blocks)
        lo = 0 if t < layers - 1 else 1
        for slot, src in zip(range(held), (src_a, src_b)):
            acc = complex_dot(op_ref, t, slot, lo, lo + len(blocks), x_real, x_imag)
            sum_ref[slot, t] = acc + jnp.concatenate([src[0, t], src[1, t]], axis=0).astype(F32)


def late_kernel(op_ref, sum_ref, near0, near1, far0, far1, out_a, out_b, *both, last):
    _, layers, held, _, _, _ = op_ref.shape
    row0 = lax.axis_index("row") == 0
    for t in range(layers):
        blocks = [[jnp.where(row0, for0[p, t], for1[p, t]) for p in range(2)] for for0, for1 in ((near0, near1), (far0, far1))]
        x_real, x_imag = stacked(blocks)
        sums = []
        for slot in range(held):
            acc = complex_dot(op_ref, t, slot, 0, len(blocks), x_real, x_imag)
            sums.append((acc + sum_ref[slot, t]).astype(BF16))
        if last:
            swap = swapped()
            sums = [jnp.where(swap, sums[1], sums[0]), jnp.where(swap, sums[0], sums[1])]
        lit = sums[0].shape[0] // 2
        for slot, (out, value) in enumerate(zip((out_a, out_b), sums)):
            for p in range(2):
                part = value[p * lit : (p + 1) * lit]
                out[p, t] = part
                if not last:
                    both[0][slot, p, t] = part


VMEM = pl.BlockSpec(memory_space=pltpu.VMEM)


def on_chip(kernel, out_shape, operands):
    many = isinstance(out_shape, tuple)
    return pl.pallas_call(
        kernel,
        out_shape=out_shape,
        in_specs=[VMEM] * len(operands),
        out_specs=(VMEM,) * len(out_shape) if many else VMEM,
        compiler_params=pltpu.CompilerParams(vmem_limit_bytes=16 << 20),
    )(*operands)


def load(scatter, pattern):
    parts, layers, held, width, _ = scatter.shape
    half = pltpu.VMEM((parts, layers, held, 2, width, width), BF16)
    return pl.pallas_call(
        load_kernel,
        out_shape=(half, half),
        in_specs=[pl.BlockSpec(memory_space=pltpu.HBM), pl.BlockSpec(memory_space=pltpu.SMEM)],
        out_specs=(VMEM, VMEM),
        scratch_shapes=[pltpu.VMEM(scatter.shape, BF16), pltpu.SemaphoreType.DMA((parts, layers, held))],
        compiler_params=pltpu.CompilerParams(vmem_limit_bytes=24 << 20),
        name="load",
    )(pltpu.with_memory_space_constraint(scatter, pltpu.HBM), pattern)


STARTS = ('far0', 'near0', 'far1', 'near1', 'within')


def paired(scatter, pattern, source):
    columns = lax.axis_size("dom")
    axes = ("dom", "row")
    perms = {
        "near0": to_same(near, columns, 4),
        "near1": to_other(near, columns),
        "far0": to_same(far, columns, 2),
        "far1": to_other(far, columns),
        "within": pairs_of(lambda c, r: (c, 1 - r), columns),
    }
    faces = jnp.transpose(source[0], (3, 0, 1, 2, 4))
    swap = swapped()
    src = (jnp.where(swap, faces[1], faces[0]), jnp.where(swap, faces[0], faces[1]))
    op_early, op_late = load(scatter[0], pattern[0])
    trace = jax.ShapeDtypeStruct(src[0].shape, BF16)
    _, layers, lit, width = trace.shape
    sums = jax.ShapeDtypeStruct((2, layers, 2 * lit, width), F32)
    pair = jax.ShapeDtypeStruct(faces.shape, BF16)
    own, both = src, faces
    for n in range(ITERS):
        last = n == ITERS - 1
        got = {}
        for name in STARTS:
            value = both if name == "within" else own[name.startswith("far")]
            got[name] = lax.ppermute(value, axes, perms[name])
        partial = on_chip(early_kernel, sums, (op_early, *src, both, got["within"]))
        late = functools.partial(late_kernel, last=last)
        operands = (op_late, partial, got["near0"], got["near1"], got["far0"], got["far1"])
        if last:
            own = on_chip(late, (trace, trace), operands)
        else:
            *own, both = on_chip(late, (trace, trace, pair), operands)
    return jnp.transpose(jnp.stack(own), (1, 2, 3, 0, 4))[None]


def local(scatter, pattern, source):
    if lax.axis_size("row") == 2 and lax.axis_size("dom") % 2 == 0 and scatter.shape[0] == 1:
        return paired(scatter, pattern, source)
    return general(scatter, pattern, source)


def solution(mesh):
    return jax.shard_map(
        local,
        mesh=mesh,
        in_specs=(
            P("dom", None, None, "row", None, None),
            P("dom", None, "row", None),
            P("dom", None, None, None, "row", None),
        ),
        out_specs=P("dom", None, None, None, "row", None),
        check_vma=False,
    )
```

```python
import functools

import jax
import jax.numpy as jnp
from jax import lax
from jax.experimental import pallas as pl
from jax.experimental.pallas import tpu as pltpu
from jax.sharding import PartitionSpec as P


ITERS = 8
F32 = jnp.float32
BF16 = jnp.bfloat16


def from_behind(value, axis, by):
    peers = lax.axis_size(axis)
    pairs = [(i, i + by) for i in range(peers) if 0 <= i + by < peers]
    return lax.ppermute(value, axis, pairs)


def horizontal(gathered, west_edge, east_edge):
    from_west = jnp.concatenate([west_edge[None], gathered[:-1, :, :, :, 1]], axis=0)
    from_east = jnp.concatenate([gathered[1:, :, :, :, 0], east_edge[None]], axis=0)
    return jnp.stack([from_west, from_east], axis=4)


def vertical(gathered):
    zero_layer = jnp.zeros_like(gathered[:, :, :1, :, 0])
    from_south = jnp.concatenate([zero_layer, gathered[:, :, :-1, :, 3]], axis=2)
    from_north = jnp.concatenate([gathered[:, :, 1:, :, 2], zero_layer], axis=2)
    return jnp.stack([from_south, from_north], axis=4)


def contract(operators, vectors):
    return jnp.einsum("ctfqk,ctfjk->ctjfq", operators, vectors, preferred_element_type=F32)


def apply_range(scatter, pattern, incoming):
    columns, layers, held, _ = pattern.shape
    count = incoming.shape[4]
    width = incoming.shape[5]
    weights = pattern.astype(BF16)[:, None, :, :, None, :, None]
    masked = weights * incoming[:, :, :, None, :, :, :]
    masked = masked.reshape(columns, 2, layers, held, incoming.shape[3], count * width)
    real_part = contract(scatter[:, 0], masked[:, 0]) - contract(scatter[:, 1], masked[:, 1])
    imag_part = contract(scatter[:, 0], masked[:, 1]) + contract(scatter[:, 1], masked[:, 0])
    return jnp.stack([real_part, imag_part], axis=1)


def edge_traces(gathered):
    columns = gathered.shape[0]
    west_edge = from_behind(gathered[columns - 1, :, :, :, 1], "dom", 1)
    east_edge = from_behind(gathered[0, :, :, :, 0], "dom", -1)
    return (west_edge, east_edge)


def general(scatter, pattern, source):
    outgoing = source
    for _ in range(ITERS):
        gathered = lax.all_gather(outgoing, "row", axis=4, tiled=True)
        west_edge, east_edge = edge_traces(gathered)
        incoming = jnp.concatenate(
            [horizontal(gathered, west_edge, east_edge), vertical(gathered)], axis=4
        )
        result = apply_range(scatter, pattern, incoming)
        outgoing = (result + source.astype(F32)).astype(BF16)
    return outgoing


def near(c, columns):
    return c ^ 1


def far(c, columns):
    other = c + 1 if c % 2 else c - 1
    return other if 0 <= other < columns else c


def to_same(partner, columns, stride):
    def target(c, r):
        other = partner(c, columns)
        if r == 0:
            return (other, 0) if other != c else (c, 1)
        beside = c ^ stride
        return (beside, 1) if partner(beside, columns) != beside else (beside, 0)

    return pairs_of(target, columns)


def to_other(partner, columns):
    def target(c, r):
        return (partner(c, columns), 1) if r == 0 else (c, 0)

    return pairs_of(target, columns)


def pairs_of(target, columns):
    pairs = []
    for c in range(columns):
        for r in range(2):
            to_c, to_r = target(c, r)
            pairs.append((2 * c + r, 2 * to_c + to_r))
    return pairs


def swapped():
    return (lax.axis_index("row") == 0) & (lax.axis_index("dom") % 2 == 0)


def load_kernel(scatter_ref, pattern_ref, early_ref, late_ref, kept_ref, raw_ref, kept_sem, sems):
    parts, layers, held, width, _ = raw_ref.shape
    columns = lax.axis_size("dom")
    column = lax.axis_index("dom")
    even = column % 2 == 0
    swap = swapped()
    inside = {0: column > 0, 1: column < columns - 1}

    def copies(t, f, p):
        spans = [(0, 4)] if 0 < t < layers - 1 else [(0, 2)]
        if t > 0 and t == layers - 1:
            spans = [(0, 3)]
        if t == 0 and t < layers - 1:
            spans.append((3, 4))
        made = []
        for k, (lo, hi) in enumerate(spans):
            cut = pl.ds(lo * width, (hi - lo) * width)
            source, target = scatter_ref.at[p, t, f, :, cut], raw_ref.at[p, t, f, :, cut]
            made.append(pltpu.make_async_copy(source, target, sems.at[p, t, f, k]))
        return made

    steps = [(t, f, p) for t in range(layers) for f in range(held) for p in range(parts)]
    fetch = pltpu.make_async_copy(pattern_ref, kept_ref, kept_sem)
    fetch.start()
    for step in steps:
        for copy in copies(*step):
            copy.start()
    fetch.wait()
    for t, f, p in steps:
        for copy in copies(t, f, p):
            copy.wait()
        slot = jnp.where(swap, 1 - f, f)
        for g in range(4):
            if (g == 3 and t == layers - 1) or (g == 2 and t == 0):
                continue
            keep = kept_ref[t, f, g] != 0
            if g in inside:
                keep = keep & inside[g]
            if g >= 2:
                ref, block = early_ref, 3 - g
            else:
                ref, block = late_ref, jnp.where(even, 1 - g, g)
            tile = raw_ref[p, t, f, :, g * width : (g + 1) * width].T
            ref[p, t, slot, block] = jnp.where(keep, tile, jnp.zeros_like(tile))


def complex_dot(op_ref, t, slot, lo, hi, x_real, x_imag):
    width = op_ref.shape[-1]
    acc = jnp.dot(x_real, op_ref[0, t, slot, lo:hi].reshape(-1, width), preferred_element_type=F32)
    return acc + jnp.dot(x_imag, op_ref[1, t, slot, lo:hi].reshape(-1, width), preferred_element_type=F32)


def stacked(blocks):
    x_real = jnp.concatenate([jnp.concatenate([re, im], axis=0) for re, im in blocks], axis=1)
    x_imag = jnp.concatenate([jnp.concatenate([-im, re], axis=0) for re, im in blocks], axis=1)
    return x_real, x_imag


def early_kernel(op_ref, src_a, src_b, own, other, sum_ref):
    _, layers, held, _, _, _ = op_ref.shape
    row0 = lax.axis_index("row") == 0
    for t in range(layers):
        blocks = []
        if t < layers - 1:
            blocks.append([jnp.where(row0, other[0, p, t + 1], own[0, p, t + 1]) for p in range(2)])
        if t > 0:
            blocks.append([jnp.where(row0, other[1, p, t - 1], own[1, p, t - 1]) for p in range(2)])
        x_real, x_imag = stacked(blocks)
        lo = 0 if t < layers - 1 else 1
        for slot, src in zip(range(held), (src_a, src_b)):
            acc = complex_dot(op_ref, t, slot, lo, lo + len(blocks), x_real, x_imag)
            sum_ref[slot, t] = acc + jnp.concatenate([src[0, t], src[1, t]], axis=0).astype(F32)


def late_kernel(op_ref, sum_ref, near0, near1, far0, far1, *outs, last):
    _, layers, held, _, _, _ = op_ref.shape
    row0 = lax.axis_index("row") == 0
    for t in range(layers):
        blocks = [[jnp.where(row0, for0[p, t], for1[p, t]) for p in range(2)] for for0, for1 in ((near0, near1), (far0, far1))]
        x_real, x_imag = stacked(blocks)
        sums = []
        for slot in range(held):
            acc = complex_dot(op_ref, t, slot, 0, len(blocks), x_real, x_imag)
            sums.append((acc + sum_ref[slot, t]).astype(BF16))
        if last:
            swap = swapped()
            sums = [jnp.where(swap, sums[1], sums[0]), jnp.where(swap, sums[0], sums[1])]
        lit = sums[0].shape[0] // 2
        if last:
            for p in range(2):
                faces = [value[p * lit : (p + 1) * lit] for value in sums]
                outs[0][p, t] = jnp.stack(faces, axis=1)
            continue
        out_a, out_b, both = outs
        for slot, (out, value) in enumerate(zip((out_a, out_b), sums)):
            for p in range(2):
                part = value[p * lit : (p + 1) * lit]
                out[p, t] = part
                both[slot, p, t] = part


VMEM = pl.BlockSpec(memory_space=pltpu.VMEM)


def on_chip(kernel, out_shape, operands):
    many = isinstance(out_shape, tuple)
    return pl.pallas_call(
        kernel,
        out_shape=out_shape,
        in_specs=[VMEM] * len(operands),
        out_specs=(VMEM,) * len(out_shape) if many else VMEM,
        compiler_params=pltpu.CompilerParams(vmem_limit_bytes=16 << 20),
    )(*operands)


def load(scatter, pattern):
    parts, layers, held, width, _ = scatter.shape
    half = pltpu.VMEM((parts, layers, held, 2, width, width), BF16)
    hbm = pl.BlockSpec(memory_space=pltpu.HBM)
    return pl.pallas_call(
        load_kernel,
        out_shape=(half, half),
        in_specs=[hbm, hbm],
        out_specs=(VMEM, VMEM),
        scratch_shapes=[
            pltpu.SMEM(pattern.shape, jnp.int32),
            pltpu.VMEM(scatter.shape, BF16),
            pltpu.SemaphoreType.DMA(()),
            pltpu.SemaphoreType.DMA((parts, layers, held, 2)),
        ],
        compiler_params=pltpu.CompilerParams(vmem_limit_bytes=24 << 20),
        name="load",
    )(pltpu.with_memory_space_constraint(scatter, pltpu.HBM), pltpu.with_memory_space_constraint(pattern, pltpu.HBM))


STARTS = ('far0', 'near0', 'far1', 'near1', 'within')


def paired(scatter, pattern, source):
    columns = lax.axis_size("dom")
    axes = ("dom", "row")
    perms = {
        "near0": to_same(near, columns, 4),
        "near1": to_other(near, columns),
        "far0": to_same(far, columns, 2),
        "far1": to_other(far, columns),
        "within": pairs_of(lambda c, r: (c, 1 - r), columns),
    }
    faces = jnp.transpose(source[0], (3, 0, 1, 2, 4))
    swap = swapped()
    src = (jnp.where(swap, faces[1], faces[0]), jnp.where(swap, faces[0], faces[1]))
    op_early, op_late = load(scatter[0], pattern[0])
    trace = jax.ShapeDtypeStruct(src[0].shape, BF16)
    _, layers, lit, width = trace.shape
    sums = jax.ShapeDtypeStruct((2, layers, 2 * lit, width), F32)
    pair = jax.ShapeDtypeStruct(faces.shape, BF16)
    own, both = src, faces
    for n in range(ITERS):
        last = n == ITERS - 1
        got = {}
        for name in STARTS:
            value = both if name == "within" else own[name.startswith("far")]
            got[name] = lax.ppermute(value, axes, perms[name])
        partial = on_chip(early_kernel, sums, (op_early, *src, both, got["within"]))
        late = functools.partial(late_kernel, last=last)
        operands = (op_late, partial, got["near0"], got["near1"], got["far0"], got["far1"])
        if last:
            out = jax.ShapeDtypeStruct(source.shape[1:], BF16)
            return on_chip(late, out, operands)[None]
        else:
            *own, both = on_chip(late, (trace, trace, pair), operands)


def local(scatter, pattern, source):
    columns_fit = scatter.shape[0] == 1 and lax.axis_size("dom") % 8 == 0
    if lax.axis_size("row") == 2 and columns_fit and scatter.shape[2] > 1:
        return paired(scatter, pattern, source)
    return general(scatter, pattern, source)


def solution(mesh):
    return jax.shard_map(
        local,
        mesh=mesh,
        in_specs=(
            P("dom", None, None, "row", None, None),
            P("dom", None, "row", None),
            P("dom", None, None, None, "row", None),
        ),
        out_specs=P("dom", None, None, None, "row", None),
        check_vma=False,
    )
```
